32 devices in a mesh: rows: 4 (over y, x), cols: 8 (over z, core).
Axes of the slice: x: 2, y: 2, z: 4, core: 2. Of those that a mesh axis runs over, the one named last changes fastest.
Arguments:
- weight: float32 [3072, 16384], P(('rows', 'cols')), may hold values from -6 to 6
- factor_panel: float32 [4, 8, 512, 1024], P(None, 'cols'), may hold values from -0.1875 to 0.1875
- diag_inverse: float32 [2, 512, 512], P(None, 'rows'), may hold values from -2 to 2, as said below
Outputs:
- whitened: float32 [3072, 4, 8, 512], P('rows', None, 'cols')
The draws below stay inside these ranges and needn't reach their ends.
Inputs may be any that keep to these rules, and one draw needn't show every extreme that they name: `diag_inverse`: each of the two blocks is lower triangular with diagonal entries between 0.5 and 2.
All inputs are finite; a program needn't handle non-finite values.
Results may differ from the reference program's by a relative error of at most 0.00007.
Values sent between devices are 32-bit elements; how exact they have to be, the bound alone decides.
A program may use at most 64 MiB of HBM per device.

```python
import math
import jax
import jax.numpy as jnp
from jax import lax

D = 16384
BLOCK = 512
R = 3072
CYC = 4
N_COLS = 8


def draw_diag_inverse(key, part):
    first_key, second_key = jax.random.split(jax.random.fold_in(key, 7))
    spread = jax.random.normal(first_key, (2, BLOCK, BLOCK), jnp.float32)
    spread = jnp.clip(spread, -6.0, 6.0) / math.sqrt(BLOCK)
    diagonal = jnp.exp(jax.random.uniform(second_key, (2, BLOCK), jnp.float32, math.log(0.5), math.log(2.0)))
    identity = jnp.eye(BLOCK, dtype=jnp.float32)
    return jnp.tril(spread, -1) + diagonal[:, :, None] * identity[None]


def shard_levels(stream_key, dims, cuts, smallest, high):
    loudness = 1.0
    for position, parts in cuts:
        steps = jax.random.uniform(jax.random.fold_in(jax.random.fold_in(stream_key, 6), position), (parts,), jnp.float32, smallest / len(cuts), high / len(cuts))
        loudness = loudness * jnp.repeat(jnp.exp(steps), dims[position] // parts).reshape((-1,) + (1,) * (len(dims) - 1 - position))
    return loudness


def noise(rng, shape, deviation, most, shards=(), kind=jnp.bfloat16):
    factor_of = shard_levels(rng, shape, shards, -0.22, 0.18) if shards else 1.0
    result = jax.random.normal(rng, shape, jnp.float32) * deviation * factor_of
    return jnp.minimum(jnp.maximum(result, -most), most).astype(kind)


def setup_inputs(seed: int = 0) -> dict:
    key_list = jax.random.split(jax.random.key(seed), 4)
    weight = noise(key_list[0], (R, D), 1.0, 6.0, ((0, 32),), jnp.float32)
    factor_panel = noise(key_list[1], (CYC, N_COLS, BLOCK, 2 * BLOCK), (2 * BLOCK) ** -0.5, 0.1875, ((1, 8),), jnp.float32)
    diag_inverse = draw_diag_inverse(jax.random.fold_in(key_list[3], 71), 0)
    return dict(weight=weight, factor_panel=factor_panel, diag_inverse=diag_inverse)


def reference(weight, factor_panel, diag_inverse):
    high = lax.Precision.HIGHEST
    blocks = weight.reshape(R, CYC * N_COLS, BLOCK)
    panel = factor_panel.reshape(CYC * N_COLS, BLOCK, 2 * BLOCK)
    solved_first = jnp.dot(blocks[:, 0], diag_inverse[0].T, precision=high)
    updated = blocks - jnp.einsum("rk,jik->rji", solved_first, panel[:, :, :BLOCK], precision=high)
    solved_second = jnp.dot(updated[:, 1], diag_inverse[1].T, precision=high)
    updated = updated - jnp.einsum("rk,jik->rji", solved_second, panel[:, :, BLOCK:], precision=high)
    updated = updated.at[:, 0].set(solved_first).at[:, 1].set(solved_second)
    return updated.reshape(R, CYC, N_COLS, BLOCK)
```

```python
import functools

import jax
import jax.numpy as jnp
from jax import lax
from jax.experimental import pallas as pl
from jax.experimental.pallas import tpu as pltpu
from jax.sharding import PartitionSpec as P

LANES = 128
TILE = 256
SEND_CLASSES = 6
BLOCKS, LEADS, SIBLING_LEADS, HALVES, INVERSES, SHARES = range(SEND_CLASSES)
WRITES = 8
VMEM_LIMIT = 50 * 10**6


def split(x):
    high = x.astype(jnp.bfloat16)
    low = (x - high.astype(jnp.float32)).astype(jnp.bfloat16)
    return high, low


def times_transpose(left_high, left_low, right):
    right_high, right_low = split(right)
    dot = functools.partial(
        lax.dot_general,
        dimension_numbers=(((1,), (1,)), ((), ())),
        preferred_element_type=jnp.float32,
    )
    return dot(left_high, right_high) + (dot(left_high, right_low) + dot(left_low, right_high))


def arrived(ref, sem):
    pltpu.make_async_copy(ref, ref, sem).wait()


def kernel(
    n_rows, n_cols, weight, panel, inverse_part, stage,
    lead, land, panel_full, inverse, bridge, a_high, a_low, x_high, x_low, solved, product,
    send_sem, lead_sem, half_sem, bridge_sem, inverse_sem, land_sem, panel_sem, present_sem, rows_sem,
):
    row, me = lax.axis_index("rows"), lax.axis_index("cols")
    chips = n_cols // 2
    z, core = me // 2, me % 2
    sibling = me + 1 - 2 * core
    part = weight.shape[0]
    cycles, block = panel.shape[0], panel.shape[2]
    share = block // n_rows
    half = share // 2
    others = n_rows - 1
    width = cycles * block // LANES

    barrier = pltpu.get_barrier_semaphore()
    has_lower, has_upper = z > 0, z < chips - 1

    def greet(sem, device):
        pl.semaphore_signal(sem, inc=1, device_id=device, device_id_type=pl.DeviceIdType.MESH)

    for other in range(2):
        pl.when(has_upper)(lambda other=other: greet(barrier, (row, 2 * (z + 1) + other)))
        pl.when(has_lower)(lambda other=other: greet(barrier, (row, 2 * (z - 1) + other)))
    greet(barrier, (row, sibling))
    def greet_rows(sem):
        for step in range(1, n_rows):
            greet(sem, ((row + step) % n_rows, me))

    even = z % 2 == 0
    pl.when(even)(lambda: greet_rows(barrier))

    def part_rows(source):
        return pl.ds(pl.multiple_of(source * part, part), part)

    def column_block(h, c):
        return pl.ds(pl.multiple_of((h * n_cols + c) * block, block), block)

    my_share = pl.ds(pl.multiple_of(row * share, share), share)

    pl.semaphore_wait(
        barrier, 1 + jnp.where(even, others, 0) + jnp.where(has_upper, 2, 0) + jnp.where(has_lower, 2, 0)
    )

    def send(condition, source, target, kind, recv_sem, device):
        def start():
            pltpu.make_async_remote_copy(
                src_ref=source,
                dst_ref=target,
                send_sem=send_sem.at[kind],
                recv_sem=recv_sem,
                device_id=device,
                device_id_type=pl.DeviceIdType.MESH,
            ).start()

        if condition is None:
            start()
        else:
            pl.when(condition)(start)

    def send_lead(condition, source_id, target_col, from_weight=False):
        source = weight.at[:, pl.ds(0, 2 * block)] if from_weight else lead.at[part_rows(source_id), :]
        kind = SIBLING_LEADS if target_col is sibling else LEADS
        send(condition, source, lead.at[part_rows(source_id), :], kind, lead_sem.at[source_id], (row, target_col))

    def half_rows(which):
        return pl.ds(pl.multiple_of(row * share + which * half, half), half)

    def send_half(condition, which, target_col, from_panel=False):
        rows = half_rows(which)
        source = panel.at[0, 0, rows, pl.ds(0, block)] if from_panel else bridge.at[rows, :]
        send(condition, source, bridge.at[rows, :], HALVES, half_sem.at[which], (row, target_col))

    def send_blocks(condition, target_col):
        for h in range(cycles):
            needed = condition
            if h == 0:
                needed = target_col > 1 if condition is None else condition & (target_col > 1)
            send(
                needed,
                weight.at[:, column_block(h, target_col)],
                land.at[h, part_rows(me), :],
                BLOCKS,
                land_sem.at[me, h // (cycles - 1)],
                (row, target_col),
            )

    send_lead(z < chips - 1, me, me + 2, True)
    send_lead(z > 0, me, me - 2, True)
    send_half(me == 1, 0, sibling, True)
    send_half(me == 1, 1, me + 2, True)
    send_half(me == 1, 1, sibling, True)
    send_lead(None, me, sibling, True)

    def forward(distance):
        left, right = me - 2 * distance, me + 2 * distance
        has_left, has_right = z >= distance, z + distance < chips

        pl.when(has_left)(lambda: arrived(lead.at[part_rows(left), :], lead_sem.at[left]))
        send_lead(has_left & (z < chips - 1), left, me + 2)
        send_lead(has_left, left, sibling)
        carries = z == distance
        pl.when(carries)(lambda: arrived(bridge.at[half_rows(core), :], half_sem.at[core]))
        send_half(carries & (z < chips - 1), core, me + 2)
        send_half(carries, core, sibling)
        pl.when(has_right)(lambda: arrived(lead.at[part_rows(right), :], lead_sem.at[right]))
        send_lead(has_right & (z > 0), right, me - 2)
        send_lead(has_right, right, sibling)

    def rest_of_inputs():
        pltpu.make_async_copy(weight.at[:, pl.ds(0, 2 * block)], lead.at[part_rows(me), :], lead_sem.at[me]).start()
        pltpu.make_async_copy(inverse_part, inverse.at[:, my_share, :], inverse_sem.at[0]).start()

        for which in range(2):
            own_half = pltpu.make_async_copy(
                panel.at[0, 0, half_rows(which), pl.ds(0, block)], bridge.at[half_rows(which), :], half_sem.at[which]
            )
            pl.when(me == 1)(own_half.start)
        for h in range(cycles):
            own = pltpu.make_async_copy(
                weight.at[:, column_block(h, me)], land.at[h, part_rows(me), :], land_sem.at[me, h // (cycles - 1)]
            )
            if h == 0:
                pl.when(me > 1)(own.start)
            else:
                own.start()
            pltpu.make_async_copy(panel.at[h, 0], panel_full.at[h], panel_sem.at[0]).start()
        pl.when(me == 0)(lambda: arrived(bridge.at[half_rows(0), :], half_sem.at[0]))
        send_half(me == 0, 0, me + 2)

    def meet_rows():
        below = even & has_upper
        pl.when(below)(lambda: greet_rows(rows_sem.at[0]))
        pl.when(below)(lambda: pl.semaphore_wait(rows_sem.at[0], others))
        pl.when(below)(lambda: greet(rows_sem.at[1], (row, me + 2)))
        pl.when(z % 2 == 1)(lambda: pl.semaphore_wait(rows_sem.at[1], 1))
        for step in range(1, n_rows):
            send(
                None,
                inverse_part,
                inverse.at[:, my_share, :],
                INVERSES,
                inverse_sem.at[0],
                ((row + step) % n_rows, me),
            )

    def tell(distance):
        if distance < chips - 1:
            pl.when((z >= distance) & has_upper)(lambda: greet(present_sem.at[0, distance + 1], (row, me + 2)))
            pl.when((z + distance < chips) & has_lower)(
                lambda: greet(present_sem.at[1, distance + 1], (row, me - 2))
            )

    def meet_far():
        tell(1)
        for distance in range(2, chips):
            pl.when(z >= distance)(lambda: pl.semaphore_wait(present_sem.at[0, distance], 1))
            pl.when(z + distance < chips)(lambda: pl.semaphore_wait(present_sem.at[1, distance], 1))
            tell(distance)

    turn = 0
    for distance in range(1, chips):
        for other in range(2):
            if turn == 1:
                send_blocks(None, sibling)
            if turn == 2:
                meet_far()
            for side in (1, -1):
                chip = z + side * distance
                exists = chip < chips if side == 1 else chip >= 0
                send_blocks(exists, 2 * chip + (core + other) % 2)
            if turn == 0:
                rest_of_inputs()
                meet_rows()
            turn += 1
            if turn < chips:
                forward(turn)

    pl.when((z > 0) | (me == 0))(lambda: arrived(bridge.at[half_rows(1 - core), :], half_sem.at[1 - core]))
    for which in range(2):
        pl.when(me == 1)(lambda which=which: arrived(bridge.at[half_rows(which), :], half_sem.at[which]))
    for step in range(1, n_rows):
        send(
            None,
            bridge.at[my_share, :],
            bridge.at[my_share, :],
            SHARES,
            bridge_sem.at[0],
            ((row + step) % n_rows, me),
        )

    arrived(lead.at[part_rows(me), :], lead_sem.at[me])
    for chip in range(chips):
        source = 2 * chip + 1 - core
        arrived(lead.at[part_rows(source), :], lead_sem.at[source])
    arrived(inverse, inverse_sem.at[0])

    @pl.loop(0, n_cols)
    def _(source):
        rows = part_rows(source)
        a_high[rows, :], a_low[rows, :] = split(lead[rows, :block])

    def tile(index, base=0):
        return pl.ds(pl.multiple_of(base + index * TILE, TILE), TILE)

    def solve(which):
        @pl.loop(0, block // TILE)
        def _(index):
            value = times_transpose(a_high[...], a_low[...], inverse[which, tile(index), :])
            columns = tile(index, which * block)
            solved[:, columns] = value
            x_high[:, columns], x_low[:, columns] = split(value)

    solve(0)
    arrived(bridge.at[pl.ds(0, others * share), :], bridge_sem.at[0])

    @pl.loop(0, block // TILE)
    def _(index):
        value = lead[:, tile(index, block)] - times_transpose(
            x_high[:, :block], x_low[:, :block], bridge[tile(index), :]
        )
        a_high[:, tile(index)], a_low[:, tile(index)] = split(value)

    solve(1)
    arrived(panel_full, panel_sem.at[0])

    @pl.loop(0, cycles)
    def _(h):
        @pl.loop(0, block // TILE)
        def _(index):
            product[h, :, tile(index)] = times_transpose(x_high[...], x_low[...], panel_full[h, tile(index), :])

    reach = jnp.minimum(z, chips - 1 - z)
    far_side = jnp.where(z < chips - 1 - z, 1, -1)

    @pl.loop(0, n_cols)
    def _(position):
        place = position // 2
        near = (place + 1) // 2 * (2 * (place % 2) - 1)
        far = (place - reach) * far_side
        chip = z + jnp.where(place <= 2 * reach, near, far)
        source = 2 * chip + (core + position) % 2
        rows = part_rows(source)

        def store(h, value):
            for q in range(block // LANES):
                first = source * (part * width) + (h * (block // LANES) + q)
                stage[pl.ds(first, part, stride=width), :] = value[:, q * LANES : (q + 1) * LANES]

        def landed(first, count):
            part_of = land.at[pl.ds(first, count), rows, :]
            arrived(part_of, land_sem.at[source, first // (cycles - 1)])

        def update(h):
            store(h, land[h, rows, :] - product[h, rows, :])

        pl.when(me > 1)(lambda: landed(0, cycles - 1))
        if cycles > 2:
            pl.when(me <= 1)(lambda: landed(1, cycles - 2))
        pl.when(me == 0)(lambda: store(0, solved[rows, :block]))
        pl.when(me == 1)(lambda: store(0, solved[rows, block:]))
        pl.when(me > 1)(lambda: update(0))
        for h in range(1, cycles):
            if h == cycles - 1:
                landed(h, 1)
            update(h)

    def left(kind, condition, view):
        pl.when(condition)(lambda: arrived(view, send_sem.at[kind]))

    def blocks_wide(count):
        return weight.at[:, pl.ds(0, count * block)]

    def bridge_rows(count):
        return bridge.at[pl.ds(0, count), :]

    count = (n_cols - 1) * cycles
    left(BLOCKS, me > 1, blocks_wide(count - 2))
    left(BLOCKS, me <= 1, blocks_wide(count - 1))
    inner = has_lower & has_upper
    left(LEADS, inner, blocks_wide(2 * (chips + 1)))
    left(LEADS, jnp.logical_not(inner), blocks_wide(2))
    arrived(blocks_wide(2 * chips), send_sem.at[SIBLING_LEADS])
    left(HALVES, me == 1, bridge_rows(3 * half))
    left(HALVES, (me == 0) | (z == chips - 1), bridge_rows(half))
    left(HALVES, inner, bridge_rows(2 * half))
    arrived(inverse.at[:, pl.ds(0, others * share), :], send_sem.at[INVERSES])
    arrived(bridge_rows(others * share), send_sem.at[SHARES])


def write_out(staged, out, sem):
    rows = staged.shape[0] // WRITES
    copies = [
        pltpu.make_async_copy(staged.at[pl.ds(i * rows, rows), :], out.at[pl.ds(i * rows, rows), :], sem.at[i])
        for i in range(WRITES)
    ]
    for copy in copies:
        copy.start()
    for copy in copies:
        copy.wait()


def solution(mesh):
    n_rows, n_cols = mesh.shape["rows"], mesh.shape["cols"]

    def per_device(weight, factor_panel, diag_inverse):
        part = weight.shape[0]
        cycles, _, block, depth = factor_panel.shape
        group = n_cols * part
        width = cycles * block // LANES
        vmem = pltpu.VMEM
        f32, bf16 = jnp.float32, jnp.bfloat16
        result = pl.pallas_call(
            functools.partial(kernel, n_rows, n_cols),
            out_shape=pltpu.VMEM((group * width, LANES), f32),
            in_specs=[pl.BlockSpec(memory_space=pltpu.HBM)] * 3,
            out_specs=pl.BlockSpec(memory_space=pltpu.VMEM),
            scratch_shapes=[
                vmem((group, 2 * block), f32),
                vmem((cycles, group, block), f32),
                vmem((cycles, block, depth), f32),
                vmem((2, block, block), f32),
                vmem((block, block), f32),
                vmem((group, block), bf16),
                vmem((group, block), bf16),
                vmem((group, depth), bf16),
                vmem((group, depth), bf16),
                vmem((group, depth), f32),
                vmem((cycles, group, block), f32),
                pltpu.SemaphoreType.DMA((SEND_CLASSES,)),
                pltpu.SemaphoreType.DMA((n_cols,)),
                pltpu.SemaphoreType.DMA((2,)),
                pltpu.SemaphoreType.DMA((1,)),
                pltpu.SemaphoreType.DMA((1,)),
                pltpu.SemaphoreType.DMA((n_cols, 2)),
                pltpu.SemaphoreType.DMA((1,)),
                pltpu.SemaphoreType.REGULAR((2, n_cols // 2)),
                pltpu.SemaphoreType.REGULAR((2,)),
            ],
            compiler_params=pltpu.CompilerParams(
                collective_id=0, has_side_effects=True, vmem_limit_bytes=VMEM_LIMIT
            ),
        )(weight, factor_panel, diag_inverse)
        result = pl.pallas_call(
            write_out,
            out_shape=jax.ShapeDtypeStruct(result.shape, f32),
            in_specs=[pl.BlockSpec(memory_space=pltpu.VMEM)],
            out_specs=pl.BlockSpec(memory_space=pltpu.HBM),
            scratch_shapes=[pltpu.SemaphoreType.DMA((WRITES,))],
            compiler_params=pltpu.CompilerParams(vmem_limit_bytes=2**20),
        )(result)
        return result.reshape(group, cycles, 1, block)

    placed = (P(("rows", "cols"), None), P(None, "cols", None, None), P(None, "rows", None))
    return jax.shard_map(
        per_device,
        mesh=mesh,
        in_specs=placed,
        out_specs=P("rows", None, "cols", None),
        check_vma=False,
    )
```

```python
import functools

import jax
import jax.numpy as jnp
from jax import lax
from jax.experimental import pallas as pl
from jax.experimental.pallas import tpu as pltpu
from jax.sharding import PartitionSpec as P

TILE = 256
SEND_CLASSES = 6
BLOCKS, LEADS, SIBLING_LEADS, HALVES, INVERSES, SHARES = range(SEND_CLASSES)
WRITES = 2
VMEM_LIMIT = 50 * 10**6


def split(x):
    high = x.astype(jnp.bfloat16)
    low = (x - high.astype(jnp.float32)).astype(jnp.bfloat16)
    return high, low


def times_transpose(left_high, left_low, right):
    right_high, right_low = split(right)
    dot = functools.partial(
        lax.dot_general,
        dimension_numbers=(((1,), (1,)), ((), ())),
        preferred_element_type=jnp.float32,
    )
    return dot(left_high, right_high) + (dot(left_high, right_low) + dot(left_low, right_high))


def arrived(ref, sem):
    pltpu.make_async_copy(ref, ref, sem).wait()


def kernel(
    n_rows, n_cols, weight, panel, inverse_part, stage,
    lead, land, panel_full, inverse, bridge, a_high, a_low, x_high, x_low, solved, product,
    send_sem, lead_sem, half_sem, bridge_sem, inverse_sem, land_sem, panel_sem, present_sem, rows_sem,
):
    row, me = lax.axis_index("rows"), lax.axis_index("cols")
    chips = n_cols // 2
    z, core = me // 2, me % 2
    sibling = me + 1 - 2 * core
    part = weight.shape[0]
    cycles, block = panel.shape[0], panel.shape[2]
    share = block // n_rows
    half = share // 2
    others = n_rows - 1

    barrier = pltpu.get_barrier_semaphore()
    has_lower, has_upper = z > 0, z < chips - 1

    def greet(sem, device):
        pl.semaphore_signal(sem, inc=1, device_id=device, device_id_type=pl.DeviceIdType.MESH)

    for other in range(2):
        pl.when(has_upper)(lambda other=other: greet(barrier, (row, 2 * (z + 1) + other)))
        pl.when(has_lower)(lambda other=other: greet(barrier, (row, 2 * (z - 1) + other)))
    greet(barrier, (row, sibling))
    def greet_rows(sem):
        for step in range(1, n_rows):
            greet(sem, ((row + step) % n_rows, me))

    even = z % 2 == 0
    pl.when(even)(lambda: greet_rows(barrier))

    def part_rows(source):
        return pl.ds(pl.multiple_of(source * part, part), part)

    def column_block(h, c):
        return pl.ds(pl.multiple_of((h * n_cols + c) * block, block), block)

    my_share = pl.ds(pl.multiple_of(row * share, share), share)

    pl.semaphore_wait(
        barrier, 1 + jnp.where(even, others, 0) + jnp.where(has_upper, 2, 0) + jnp.where(has_lower, 2, 0)
    )

    def send(condition, source, target, kind, recv_sem, device):
        def start():
            pltpu.make_async_remote_copy(
                src_ref=source,
                dst_ref=target,
                send_sem=send_sem.at[kind],
                recv_sem=recv_sem,
                device_id=device,
                device_id_type=pl.DeviceIdType.MESH,
            ).start()

        if condition is None:
            start()
        else:
            pl.when(condition)(start)

    def send_lead(condition, source_id, target_col, from_weight=False):
        source = weight.at[:, pl.ds(0, 2 * block)] if from_weight else lead.at[part_rows(source_id), :]
        kind = SIBLING_LEADS if target_col is sibling else LEADS
        send(condition, source, lead.at[part_rows(source_id), :], kind, lead_sem.at[source_id], (row, target_col))

    def half_rows(which):
        return pl.ds(pl.multiple_of(row * share + which * half, half), half)

    def send_half(condition, which, target_col, from_panel=False):
        rows = half_rows(which)
        source = panel.at[0, 0, rows, pl.ds(0, block)] if from_panel else bridge.at[rows, :]
        send(condition, source, bridge.at[rows, :], HALVES, half_sem.at[which], (row, target_col))

    def send_blocks(condition, target_col):
        for h in range(cycles):
            needed = condition
            if h == 0:
                needed = target_col > 1 if condition is None else condition & (target_col > 1)
            send(
                needed,
                weight.at[:, column_block(h, target_col)],
                land.at[h, part_rows(me), :],
                BLOCKS,
                land_sem.at[me],
                (row, target_col),
            )

    send_lead(z < chips - 1, me, me + 2, True)
    send_lead(z > 0, me, me - 2, True)
    send_half(me == 1, 0, sibling, True)
    send_half(me == 1, 1, me + 2, True)
    send_half(me == 1, 1, sibling, True)
    send_lead(None, me, sibling, True)

    def forward(distance):
        left, right = me - 2 * distance, me + 2 * distance
        has_left, has_right = z >= distance, z + distance < chips

        pl.when(has_left)(lambda: arrived(lead.at[part_rows(left), :], lead_sem.at[left]))
        send_lead(has_left & (z < chips - 1), left, me + 2)
        send_lead(has_left, left, sibling)
        carries = z == distance
        pl.when(carries)(lambda: arrived(bridge.at[half_rows(core), :], half_sem.at[core]))
        send_half(carries & (z < chips - 1), core, me + 2)
        send_half(carries, core, sibling)
        pl.when(has_right)(lambda: arrived(lead.at[part_rows(right), :], lead_sem.at[right]))
        send_lead(has_right & (z > 0), right, me - 2)
        send_lead(has_right, right, sibling)

    def rest_of_inputs():
        pltpu.make_async_copy(weight.at[:, pl.ds(0, 2 * block)], lead.at[part_rows(me), :], lead_sem.at[me]).start()
        pltpu.make_async_copy(inverse_part, inverse.at[:, my_share, :], inverse_sem.at[0]).start()

        for which in range(2):
            own_half = pltpu.make_async_copy(
                panel.at[0, 0, half_rows(which), pl.ds(0, block)], bridge.at[half_rows(which), :], half_sem.at[which]
            )
            pl.when(me == 1)(own_half.start)
        for h in range(cycles):
            own = pltpu.make_async_copy(
                weight.at[:, column_block(h, me)], land.at[h, part_rows(me), :], land_sem.at[me]
            )
            if h == 0:
                pl.when(me > 1)(own.start)
            else:
                own.start()
            pltpu.make_async_copy(panel.at[h, 0], panel_full.at[h], panel_sem.at[0]).start()
        pl.when(me == 0)(lambda: arrived(bridge.at[half_rows(0), :], half_sem.at[0]))
        send_half(me == 0, 0, me + 2)

    def meet_rows():
        below = even & has_upper
        pl.when(below)(lambda: greet_rows(rows_sem.at[0]))
        pl.when(below)(lambda: pl.semaphore_wait(rows_sem.at[0], others))
        pl.when(below)(lambda: greet(rows_sem.at[1], (row, me + 2)))
        pl.when(z % 2 == 1)(lambda: pl.semaphore_wait(rows_sem.at[1], 1))
        for step in range(1, n_rows):
            send(
                None,
                inverse_part,
                inverse.at[:, my_share, :],
                INVERSES,
                inverse_sem.at[0],
                ((row + step) % n_rows, me),
            )

    def tell(distance):
        if distance < chips - 1:
            pl.when((z >= distance) & has_upper)(lambda: greet(present_sem.at[0, distance - 1], (row, me + 2)))
            pl.when((z + distance < chips) & has_lower)(
                lambda: greet(present_sem.at[1, distance - 1], (row, me - 2))
            )

    def meet_far():
        tell(1)
        for distance in range(2, chips):
            pl.when(z >= distance)(lambda: pl.semaphore_wait(present_sem.at[0, distance - 2], 1))
            pl.when(z + distance < chips)(lambda: pl.semaphore_wait(present_sem.at[1, distance - 2], 1))
            tell(distance)

    turn = 0
    for distance in range(1, chips):
        for other in range(2):
            if turn == 1:
                send_blocks(None, sibling)
            if turn == 2:
                meet_far()
            for side in (1, -1):
                chip = z + side * distance
                exists = chip < chips if side == 1 else chip >= 0
                send_blocks(exists, 2 * chip + (core + other) % 2)
            if turn == 0:
                rest_of_inputs()
                meet_rows()
            turn += 1
            if turn < chips:
                forward(turn)

    pl.when((z > 0) | (me == 0))(lambda: arrived(bridge.at[half_rows(1 - core), :], half_sem.at[1 - core]))
    for which in range(2):
        pl.when(me == 1)(lambda which=which: arrived(bridge.at[half_rows(which), :], half_sem.at[which]))
    for step in range(1, n_rows):
        send(
            None,
            bridge.at[my_share, :],
            bridge.at[my_share, :],
            SHARES,
            bridge_sem.at[0],
            ((row + step) % n_rows, me),
        )

    arrived(lead.at[part_rows(me), :], lead_sem.at[me])
    for chip in range(chips):
        source = 2 * chip + 1 - core
        arrived(lead.at[part_rows(source), :], lead_sem.at[source])
    arrived(inverse, inverse_sem.at[0])

    @pl.loop(0, n_cols)
    def _(source):
        rows = part_rows(source)
        a_high[rows, :], a_low[rows, :] = split(lead[rows, :block])

    def tile(index, base=0):
        return pl.ds(pl.multiple_of(base + index * TILE, TILE), TILE)

    def solve(which):
        @pl.loop(0, block // TILE)
        def _(index):
            value = times_transpose(a_high[...], a_low[...], inverse[which, tile(index), :])
            columns = tile(index, which * block)
            solved[:, columns] = value
            x_high[:, columns], x_low[:, columns] = split(value)

    solve(0)
    arrived(bridge.at[pl.ds(0, others * share), :], bridge_sem.at[0])

    @pl.loop(0, block // TILE)
    def _(index):
        value = lead[:, tile(index, block)] - times_transpose(
            x_high[:, :block], x_low[:, :block], bridge[tile(index), :]
        )
        a_high[:, tile(index)], a_low[:, tile(index)] = split(value)

    solve(1)
    arrived(panel_full, panel_sem.at[0])

    @pl.loop(0, cycles)
    def _(h):
        @pl.loop(0, block // TILE)
        def _(index):
            product[h, :, tile(index)] = times_transpose(x_high[...], x_low[...], panel_full[h, tile(index), :])

    reach = jnp.minimum(z, chips - 1 - z)
    far_side = jnp.where(z < chips - 1 - z, 1, -1)

    @pl.loop(0, n_cols)
    def _(position):
        place = position // 2
        near = (place + 1) // 2 * (2 * (place % 2) - 1)
        far = (place - reach) * far_side
        chip = z + jnp.where(place <= 2 * reach, near, far)
        source = 2 * chip + (core + position) % 2
        rows = part_rows(source)

        def landed(first):
            arrived(land.at[pl.ds(first, cycles - first), rows, :], land_sem.at[source])

        def store(h, value):
            stage[h, rows, :] = value

        def update(h):
            store(h, land[h, rows, :] - product[h, rows, :])

        pl.when(me > 1)(lambda: landed(0))
        pl.when(me <= 1)(lambda: landed(1))
        pl.when(me == 0)(lambda: store(0, solved[rows, :block]))
        pl.when(me == 1)(lambda: store(0, solved[rows, block:]))
        pl.when(me > 1)(lambda: update(0))
        for h in range(1, cycles):
            update(h)

    def left(kind, condition, view):
        pl.when(condition)(lambda: arrived(view, send_sem.at[kind]))

    def blocks_wide(count):
        return weight.at[:, pl.ds(0, count * block)]

    def bridge_rows(count):
        return bridge.at[pl.ds(0, count), :]

    count = (n_cols - 1) * cycles
    left(BLOCKS, me > 1, blocks_wide(count - 2))
    left(BLOCKS, me <= 1, blocks_wide(count - 1))
    inner = has_lower & has_upper
    left(LEADS, inner, blocks_wide(2 * (chips + 1)))
    left(LEADS, jnp.logical_not(inner), blocks_wide(2))
    arrived(blocks_wide(2 * chips), send_sem.at[SIBLING_LEADS])
    left(HALVES, me == 1, bridge_rows(3 * half))
    left(HALVES, (me == 0) | (z == chips - 1), bridge_rows(half))
    left(HALVES, inner, bridge_rows(2 * half))
    arrived(inverse.at[:, pl.ds(0, others * share), :], send_sem.at[INVERSES])
    arrived(bridge_rows(others * share), send_sem.at[SHARES])


def write_out(staged, out, sem):
    cycles, group, _ = staged.shape
    rows = group // WRITES
    for h in range(cycles):
        for i in range(WRITES):
            some = pl.ds(i * rows, rows)
            pltpu.make_async_copy(staged.at[h, some, :], out.at[some, h, 0, :], sem.at[0]).start()
    pltpu.make_async_copy(staged, staged, sem.at[0]).wait()


def solution(mesh):
    n_rows, n_cols = mesh.shape["rows"], mesh.shape["cols"]

    def per_device(weight, factor_panel, diag_inverse):
        part = weight.shape[0]
        cycles, _, block, depth = factor_panel.shape
        group = n_cols * part
        vmem = pltpu.VMEM
        f32, bf16 = jnp.float32, jnp.bfloat16
        result = pl.pallas_call(
            functools.partial(kernel, n_rows, n_cols),
            out_shape=pltpu.VMEM((cycles, group, block), f32),
            in_specs=[pl.BlockSpec(memory_space=pltpu.HBM)] * 3,
            out_specs=pl.BlockSpec(memory_space=pltpu.VMEM),
            scratch_shapes=[
                vmem((group, 2 * block), f32),
                vmem((cycles, group, block), f32),
                vmem((cycles, block, depth), f32),
                vmem((2, block, block), f32),
                vmem((block, block), f32),
                vmem((group, block), bf16),
                vmem((group, block), bf16),
                vmem((group, depth), bf16),
                vmem((group, depth), bf16),
                vmem((group, depth), f32),
                vmem((cycles, group, block), f32),
                pltpu.SemaphoreType.DMA((SEND_CLASSES,)),
                pltpu.SemaphoreType.DMA((n_cols,)),
                pltpu.SemaphoreType.DMA((2,)),
                pltpu.SemaphoreType.DMA((1,)),
                pltpu.SemaphoreType.DMA((1,)),
                pltpu.SemaphoreType.DMA((n_cols,)),
                pltpu.SemaphoreType.DMA((1,)),
                pltpu.SemaphoreType.REGULAR((2, n_cols // 2 - 2)),
                pltpu.SemaphoreType.REGULAR((2,)),
            ],
            compiler_params=pltpu.CompilerParams(
                collective_id=0, has_side_effects=True, vmem_limit_bytes=VMEM_LIMIT
            ),
        )(weight, factor_panel, diag_inverse)
        return pl.pallas_call(
            write_out,
            out_shape=jax.ShapeDtypeStruct((group, cycles, 1, block), f32),
            in_specs=[pl.BlockSpec(memory_space=pltpu.VMEM)],
            out_specs=pl.BlockSpec(memory_space=pltpu.HBM),
            scratch_shapes=[pltpu.SemaphoreType.DMA((1,))],
            compiler_params=pltpu.CompilerParams(vmem_limit_bytes=2**20),
        )(result)

    placed = (P(("rows", "cols"), None), P(None, "cols", None, None), P(None, "rows", None))
    return jax.shard_map(
        per_device,
        mesh=mesh,
        in_specs=placed,
        out_specs=P("rows", None, "cols", None),
        check_vma=False,
    )
```

```python
import functools

import jax
import jax.numpy as jnp
from jax import lax
from jax.experimental import pallas as pl
from jax.experimental.pallas import tpu as pltpu
from jax.sharding import PartitionSpec as P

TILE = 256
SEND_CLASSES = 6
BLOCKS, LEADS, SIBLING_LEADS, HALVES, INVERSES, SHARES = range(SEND_CLASSES)
WRITES = 2
VMEM_LIMIT = 50 * 10**6


def split(x):
    high = x.astype(jnp.bfloat16)
    low = (x - high.astype(jnp.float32)).astype(jnp.bfloat16)
    return high, low


def times_transpose(left_high, left_low, right):
    right_high, right_low = split(right)
    dot = functools.partial(
        lax.dot_general,
        dimension_numbers=(((1,), (1,)), ((), ())),
        preferred_element_type=jnp.float32,
    )
    return dot(left_high, right_high) + (dot(left_high, right_low) + dot(left_low, right_high))


def arrived(ref, sem):
    pltpu.make_async_copy(ref, ref, sem).wait()


def kernel(
    n_rows, n_cols, weight, panel, inverse_part, stage,
    lead, land, panel_full, inverse, bridge, a_high, a_low, x_high, x_low, solved, product,
    send_sem, lead_sem, half_sem, bridge_sem, inverse_sem, land_sem, panel_sem, present_sem, rows_sem,
):
    row, me = lax.axis_index("rows"), lax.axis_index("cols")
    chips = n_cols // 2
    z, core = me // 2, me % 2
    sibling = me + 1 - 2 * core
    part = weight.shape[0]
    cycles, block = panel.shape[0], panel.shape[2]
    share = block // n_rows
    split_at = share * 3 // 64 * 8
    halves = split_at, share - split_at
    others = n_rows - 1

    barrier = pltpu.get_barrier_semaphore()
    has_lower, has_upper = z > 0, z < chips - 1

    def greet(sem, device):
        pl.semaphore_signal(sem, inc=1, device_id=device, device_id_type=pl.DeviceIdType.MESH)

    for other in range(2):
        pl.when(has_upper)(lambda other=other: greet(barrier, (row, 2 * (z + 1) + other)))
        pl.when(has_lower)(lambda other=other: greet(barrier, (row, 2 * (z - 1) + other)))
    greet(barrier, (row, sibling))
    def greet_rows(sem):
        for step in range(1, n_rows):
            greet(sem, ((row + step) % n_rows, me))

    even = z % 2 == 0
    pl.when(even)(lambda: greet_rows(barrier))

    def part_rows(source):
        return pl.ds(pl.multiple_of(source * part, part), part)

    def column_block(h, c):
        return pl.ds(pl.multiple_of((h * n_cols + c) * block, block), block)

    my_share = pl.ds(pl.multiple_of(row * share, share), share)

    pl.semaphore_wait(
        barrier, 1 + jnp.where(even, others, 0) + jnp.where(has_upper, 2, 0) + jnp.where(has_lower, 2, 0)
    )

    def send(condition, source, target, kind, recv_sem, device):
        def start():
            pltpu.make_async_remote_copy(
                src_ref=source,
                dst_ref=target,
                send_sem=send_sem.at[kind],
                recv_sem=recv_sem,
                device_id=device,
                device_id_type=pl.DeviceIdType.MESH,
            ).start()

        if condition is None:
            start()
        else:
            pl.when(condition)(start)

    def send_lead(condition, source_id, target_col, from_weight=False):
        source = weight.at[:, pl.ds(0, 2 * block)] if from_weight else lead.at[part_rows(source_id), :]
        kind = SIBLING_LEADS if target_col is sibling else LEADS
        send(condition, source, lead.at[part_rows(source_id), :], kind, lead_sem.at[source_id], (row, target_col))

    def half_rows(which):
        return pl.ds(pl.multiple_of(row * share + which * split_at, 8), halves[which])

    def send_half(condition, which, target_col, from_panel=False):
        rows = half_rows(which)
        source = panel.at[0, 0, rows, pl.ds(0, block)] if from_panel else bridge.at[rows, :]
        send(condition, source, bridge.at[rows, :], HALVES, half_sem.at[which], (row, target_col))

    def send_blocks(condition, target_col):
        for h in range(cycles):
            needed = condition
            if h == 0:
                needed = target_col > 1 if condition is None else condition & (target_col > 1)
            send(
                needed,
                weight.at[:, column_block(h, target_col)],
                land.at[h, part_rows(me), :],
                BLOCKS,
                land_sem.at[me],
                (row, target_col),
            )

    send_lead(z < chips - 1, me, me + 2, True)
    send_lead(z > 0, me, me - 2, True)
    send_half(me == 1, 0, sibling, True)
    send_half(me == 1, 1, me + 2, True)
    send_half(me == 1, 1, sibling, True)
    send_lead(None, me, sibling, True)

    def forward(distance):
        left, right = me - 2 * distance, me + 2 * distance
        has_left, has_right = z >= distance, z + distance < chips

        pl.when(has_left)(lambda: arrived(lead.at[part_rows(left), :], lead_sem.at[left]))
        send_lead(has_left & (z < chips - 1), left, me + 2)
        send_lead(has_left, left, sibling)
        carries = z == distance
        for which in range(2):
            on_chain = carries & (core == which)
            pl.when(on_chain)(lambda which=which: arrived(bridge.at[half_rows(which), :], half_sem.at[which]))
            send_half(on_chain & (z < chips - 1), which, me + 2)
            send_half(on_chain, which, sibling)
        pl.when(has_right)(lambda: arrived(lead.at[part_rows(right), :], lead_sem.at[right]))
        send_lead(has_right & (z > 0), right, me - 2)
        send_lead(has_right, right, sibling)

    def rest_of_inputs():
        pltpu.make_async_copy(weight.at[:, pl.ds(0, 2 * block)], lead.at[part_rows(me), :], lead_sem.at[me]).start()
        pltpu.make_async_copy(inverse_part, inverse.at[:, my_share, :], inverse_sem.at[0]).start()

        for which in range(2):
            own_half = pltpu.make_async_copy(
                panel.at[0, 0, half_rows(which), pl.ds(0, block)], bridge.at[half_rows(which), :], half_sem.at[which]
            )
            pl.when(me == 1)(own_half.start)
        for h in range(cycles):
            own = pltpu.make_async_copy(
                weight.at[:, column_block(h, me)], land.at[h, part_rows(me), :], land_sem.at[me]
            )
            if h == 0:
                pl.when(me > 1)(own.start)
            else:
                own.start()
            pltpu.make_async_copy(panel.at[h, 0], panel_full.at[h], panel_sem.at[0]).start()
        pl.when(me == 0)(lambda: arrived(bridge.at[half_rows(0), :], half_sem.at[0]))
        send_half(me == 0, 0, me + 2)

    def meet_rows():
        below = even & has_upper
        pl.when(below)(lambda: greet_rows(rows_sem.at[0]))
        pl.when(below)(lambda: pl.semaphore_wait(rows_sem.at[0], others))
        pl.when(below)(lambda: greet(rows_sem.at[1], (row, me + 2)))
        pl.when(z % 2 == 1)(lambda: pl.semaphore_wait(rows_sem.at[1], 1))
        for step in range(1, n_rows):
            send(
                None,
                inverse_part,
                inverse.at[:, my_share, :],
                INVERSES,
                inverse_sem.at[0],
                ((row + step) % n_rows, me),
            )

    def tell(distance):
        if distance < chips - 1:
            pl.when((z >= distance) & has_upper)(lambda: greet(present_sem.at[0, distance - 1], (row, me + 2)))
            pl.when((z + distance < chips) & has_lower)(
                lambda: greet(present_sem.at[1, distance - 1], (row, me - 2))
            )

    def meet_far():
        tell(1)
        for distance in range(2, chips):
            pl.when(z >= distance)(lambda: pl.semaphore_wait(present_sem.at[0, distance - 2], 1))
            pl.when(z + distance < chips)(lambda: pl.semaphore_wait(present_sem.at[1, distance - 2], 1))
            tell(distance)

    turn = 0
    for distance in range(1, chips):
        for other in range(2):
            if turn == 1:
                send_blocks(None, sibling)
            if turn == 2:
                meet_far()
            for side in (1, -1):
                chip = z + side * distance
                exists = chip < chips if side == 1 else chip >= 0
                send_blocks(exists, 2 * chip + (core + other) % 2)
            if turn == 0:
                rest_of_inputs()
                meet_rows()
            turn += 1
            if turn < chips:
                forward(turn)

    for which in range(2):
        pending = (me == 1) | (((z > 0) | (me == 0)) & (core != which))
        pl.when(pending)(lambda which=which: arrived(bridge.at[half_rows(which), :], half_sem.at[which]))
    for step in range(1, n_rows):
        send(
            None,
            bridge.at[my_share, :],
            bridge.at[my_share, :],
            SHARES,
            bridge_sem.at[0],
            ((row + step) % n_rows, me),
        )

    arrived(lead.at[part_rows(me), :], lead_sem.at[me])
    for chip in range(chips):
        source = 2 * chip + 1 - core
        arrived(lead.at[part_rows(source), :], lead_sem.at[source])
    arrived(inverse, inverse_sem.at[0])

    @pl.loop(0, n_cols)
    def _(source):
        rows = part_rows(source)
        a_high[rows, :], a_low[rows, :] = split(lead[rows, :block])

    def tile(index, base=0):
        return pl.ds(pl.multiple_of(base + index * TILE, TILE), TILE)

    def solve(which):
        @pl.loop(0, block // TILE)
        def _(index):
            value = times_transpose(a_high[...], a_low[...], inverse[which, tile(index), :])
            columns = tile(index, which * block)
            solved[:, columns] = value
            x_high[:, columns], x_low[:, columns] = split(value)

    solve(0)
    arrived(bridge.at[pl.ds(0, others * share), :], bridge_sem.at[0])

    @pl.loop(0, block // TILE)
    def _(index):
        value = lead[:, tile(index, block)] - times_transpose(
            x_high[:, :block], x_low[:, :block], bridge[tile(index), :]
        )
        a_high[:, tile(index)], a_low[:, tile(index)] = split(value)

    solve(1)
    arrived(panel_full, panel_sem.at[0])

    @pl.loop(0, cycles)
    def _(h):
        @pl.loop(0, block // TILE)
        def _(index):
            product[h, :, tile(index)] = times_transpose(x_high[...], x_low[...], panel_full[h, tile(index), :])

    reach = jnp.minimum(z, chips - 1 - z)
    far_side = jnp.where(z < chips - 1 - z, 1, -1)

    @pl.loop(0, n_cols)
    def _(position):
        place = position // 2
        near = (place + 1) // 2 * (2 * (place % 2) - 1)
        far = (place - reach) * far_side
        chip = z + jnp.where(place <= 2 * reach, near, far)
        source = 2 * chip + (core + position) % 2
        rows = part_rows(source)

        def landed(first):
            arrived(land.at[pl.ds(first, cycles - first), rows, :], land_sem.at[source])

        def store(h, value):
            stage[h, rows, :] = value

        def update(h):
            store(h, land[h, rows, :] - product[h, rows, :])

        pl.when(me > 1)(lambda: landed(0))
        pl.when(me <= 1)(lambda: landed(1))
        pl.when(me == 0)(lambda: store(0, solved[rows, :block]))
        pl.when(me == 1)(lambda: store(0, solved[rows, block:]))
        pl.when(me > 1)(lambda: update(0))
        for h in range(1, cycles):
            update(h)

    def left(kind, condition, view):
        pl.when(condition)(lambda: arrived(view, send_sem.at[kind]))

    def blocks_wide(count):
        return weight.at[:, pl.ds(0, count * block)]

    def bridge_rows(count):
        return bridge.at[pl.ds(0, count), :]

    count = (n_cols - 1) * cycles
    left(BLOCKS, me > 1, blocks_wide(count - 2))
    left(BLOCKS, me <= 1, blocks_wide(count - 1))
    inner = has_lower & has_upper
    left(LEADS, inner, blocks_wide(2 * (chips + 1)))
    left(LEADS, jnp.logical_not(inner), blocks_wide(2))
    arrived(blocks_wide(2 * chips), send_sem.at[SIBLING_LEADS])
    left(HALVES, me == 1, bridge_rows(halves[0] + 2 * halves[1]))
    left(HALVES, me == 0, bridge_rows(halves[0]))
    for which in range(2):
        left(HALVES, (core == which) & (z == chips - 1), bridge_rows(halves[which]))
        left(HALVES, (core == which) & inner, bridge_rows(2 * halves[which]))
    arrived(inverse.at[:, pl.ds(0, others * share), :], send_sem.at[INVERSES])
    arrived(bridge_rows(others * share), send_sem.at[SHARES])


def write_out(staged, out, sem):
    cycles, group, _ = staged.shape
    rows = group // WRITES
    for h in range(cycles):
        for i in range(WRITES):
            some = pl.ds(i * rows, rows)
            pltpu.make_async_copy(staged.at[h, some, :], out.at[some, h, 0, :], sem.at[0]).start()
    pltpu.make_async_copy(staged, staged, sem.at[0]).wait()


def solution(mesh):
    n_rows, n_cols = mesh.shape["rows"], mesh.shape["cols"]

    def per_device(weight, factor_panel, diag_inverse):
        part = weight.shape[0]
        cycles, _, block, depth = factor_panel.shape
        group = n_cols * part
        vmem = pltpu.VMEM
        f32, bf16 = jnp.float32, jnp.bfloat16
        result = pl.pallas_call(
            functools.partial(kernel, n_rows, n_cols),
            out_shape=pltpu.VMEM((cycles, group, block), f32),
            in_specs=[pl.BlockSpec(memory_space=pltpu.HBM)] * 3,
            out_specs=pl.BlockSpec(memory_space=pltpu.VMEM),
            scratch_shapes=[
                vmem((group, 2 * block), f32),
                vmem((cycles, group, block), f32),
                vmem((cycles, block, depth), f32),
                vmem((2, block, block), f32),
                vmem((block, block), f32),
                vmem((group, block), bf16),
                vmem((group, block), bf16),
                vmem((group, depth), bf16),
                vmem((group, depth), bf16),
                vmem((group, depth), f32),
                vmem((cycles, group, block), f32),
                pltpu.SemaphoreType.DMA((SEND_CLASSES,)),
                pltpu.SemaphoreType.DMA((n_cols,)),
                pltpu.SemaphoreType.DMA((2,)),
                pltpu.SemaphoreType.DMA((1,)),
                pltpu.SemaphoreType.DMA((1,)),
                pltpu.SemaphoreType.DMA((n_cols,)),
                pltpu.SemaphoreType.DMA((1,)),
                pltpu.SemaphoreType.REGULAR((2, n_cols // 2 - 2)),
                pltpu.SemaphoreType.REGULAR((2,)),
            ],
            compiler_params=pltpu.CompilerParams(
                collective_id=0, has_side_effects=True, vmem_limit_bytes=VMEM_LIMIT
            ),
        )(weight, factor_panel, diag_inverse)
        return pl.pallas_call(
            write_out,
            out_shape=jax.ShapeDtypeStruct((group, cycles, 1, block), f32),
            in_specs=[pl.BlockSpec(memory_space=pltpu.VMEM)],
            out_specs=pl.BlockSpec(memory_space=pltpu.HBM),
            scratch_shapes=[pltpu.SemaphoreType.DMA((1,))],
            compiler_params=pltpu.CompilerParams(vmem_limit_bytes=2**20),
        )(result)

    placed = (P(("rows", "cols"), None), P(None, "cols", None, None), P(None, "rows", None))
    return jax.shard_map(
        per_device,
        mesh=mesh,
        in_specs=placed,
        out_specs=P("rows", None, "cols", None),
        check_vma=False,
    )
```
